128 devices in a mesh: grp: 16 (over x, y_lo, core), blk: 8 (over z, y_hi).
Axes of the slice: x: 4, y: 4 (y_hi: 2, y_lo: 2; y = y_hi * 2 + y_lo), z: 4, core: 2. Of those that a mesh axis runs over, the one named last changes fastest.
Arguments:
- nodes: float32 [16, 3, 128, 256], P('grp', None, 'blk'), may hold values from -4 to 4
- panels: float32 [16, 3, 4096], P('grp', None, 'blk'), may hold values from -4 to 4
- nu_field: float32 [16, 128, 256], P('grp', 'blk'), may hold values from 0.2 to 1.5
- vorticity: float32 [16, 128, 256], P('grp', 'blk'), may hold values from 1 to 100
- flow: float32 [16, 4, 128, 256], P('grp', None, 'blk'), may hold values from -6 to 6
- fringe_block: int32 [16384], P(('grp', 'blk')), may hold values from 0 to 31
- fringe_size: int32 [16384], P(('grp', 'blk')), may hold values from 1 to 128
- fringe_owner: int32 [16384, 1], P(('grp', 'blk')), may hold values from 0 to 127; in each aligned block of 128 rows (0 to 127, 128 to 255, ...) at most 2 rows name the same one
- fringe_cell: int32 [16384], P(('grp', 'blk')), may hold values from 0 to 15
Outputs:
- wall_distance: float32 [16, 128, 256], P('grp', 'blk')
- nu_next: float32 [16, 128, 256], P('grp', 'blk')
- offbody: float32 [2048, 5, 128], P(('grp', 'blk'))
The draws below stay inside these ranges and needn't reach their ends.
Inputs may be any that keep to these rules, and one draw needn't show every extreme that they name: `fringe_owner`: among the 128 slots of one device, at most 2 name the same owner device.
All inputs are finite; a program needn't handle non-finite values.
Results may differ from the reference program's by a relative error of at most 0.00012.
Values sent between devices are 32-bit elements; how exact they have to be, the bound alone decides.
No kernel may reach another device: no remote copies, remote signals or barrier semaphores. Data moves between devices by JAX's collectives and lax.ppermute only.
A program may use at most 64 MiB of HBM per device.

```python
import math
import jax
import jax.numpy as jnp
import numpy as np
from jax import lax

NJ = 256
PANELS_DEV = 512
BLOCK = 128
VARS = 5
CAP = 2
OB = 16
GROUPS = 16
NI = 128
PANELS = 4096
NB_DEV = 32
FR_DEV = 128
FR_ALL = 16384
OB_ALL = 2048
N_BLK = 8
DEVICES = 128


def with_ends(entries, rng, low, high):
    shape = entries.shape
    place = [jax.random.randint(jax.random.fold_in(rng, axis), (), 0, shape[axis]) for axis in range(len(shape))]
    entries = entries.at[tuple(place)].set(low)
    longest = shape.index(max(shape))
    place[longest] = (place[longest] + 1) % shape[longest]
    return entries.at[tuple(place)].set(high)


def level_of(own_key, shape, cuts, low, high):
    def one(axis_at, parts):
        heights = jax.random.uniform(jax.random.fold_in(jax.random.fold_in(own_key, 6), axis_at), (parts,), jnp.float32, low / len(cuts), high / len(cuts))
        return jnp.repeat(jnp.exp(heights), shape[axis_at] // parts).reshape((-1,) + (1,) * (len(shape) - axis_at - 1))

    level = one(*cuts[0])
    for cut in cuts[1:]:
        level = level * one(*cut)
    return level


def routed_block(own_key, own, number, rows, number_of, top, reach, lean):
    order = jax.random.permutation(own_key, number_of)
    heavy_load, ordinary = portions_of(number_of, rows * top, reach, lean, True), portions_of(number_of, rows * top, reach, lean, False)
    places = jnp.arange(number_of)

    def named(sizes, turn):
        used = int((sizes > 0).sum())
        fixed = max(1, used // 4)
        shifted = fixed + (places - fixed + turn * (used - fixed)) % max(1, number_of - fixed)
        return jnp.zeros((number_of,), jnp.int32).at[order[jnp.where(places < fixed, places, shifted)]].set(jnp.asarray(sizes, jnp.int32))

    sizes = jnp.where(number % 4 == 0, named(heavy_load, number // 4), named(ordinary, number - number // 4 - 1))
    mixed = jax.random.permutation(jax.random.fold_in(own, 3), number_of)
    source_of, sink = mixed[0:number_of // 2 * 2:2], mixed[1:number_of // 2 * 2:2]
    slack = jnp.minimum(sizes[source_of] - 1, reach - sizes[sink]) // 2
    slack = jnp.where((source_of == order[0]) | (sink == order[0]) | (sizes[sink] == 0), 0, jnp.maximum(slack, 0))
    shifted = jax.random.randint(jax.random.fold_in(own, 4), (number_of // 2,), 0, 1 << 20) % (slack + 1)
    sizes = sizes.at[source_of].add(-shifted).at[sink].add(shifted)
    items = jnp.searchsorted(jnp.cumsum(sizes), jnp.arange(rows * top), side="right").astype(jnp.int32)
    listing = items.reshape(top, rows).T
    listing = listing[jax.random.permutation(jax.random.fold_in(own, 1), rows)]
    turn = jax.random.randint(jax.random.fold_in(own, 2), (rows, 1), 0, top)
    return jnp.take_along_axis(listing, (jnp.arange(top)[None, :] + turn) % top, axis=1)


def portions_of(amount, total, limit, skew, full):
    portions = [(1 << 20) // math.isqrt(grade ** skew) + 1 for grade in range(1, amount + 1)]
    largest = limit if full else min(limit, max(-(-total // amount), total * portions[0] // sum(portions)))
    least = 1 if total - largest >= amount - 1 else 0
    given, rest = [largest] + [least] * (amount - 1), total - largest - least * (amount - 1)
    while rest > 0:
        candidates = [i for i in range(1, amount) if given[i] < largest] or [i for i in range(1, amount) if given[i] < limit]
        pool, remaining = sum([portions[i] for i in candidates]), rest
        for i in candidates:
            extra = min(limit - given[i], max(1, remaining * portions[i] // pool), rest)
            given[i] = given[i] + extra
            rest = rest - extra
    return np.array(given)


def gaussian(own_key, dims, spread, reach, pieces=(), held_as=jnp.bfloat16):
    loudness = level_of(own_key, dims, pieces, -0.22, 0.18) if pieces else 1.0
    values = jax.random.normal(own_key, dims, jnp.float32) * spread * loudness
    return jnp.minimum(jnp.maximum(values, -reach), reach).astype(held_as)


def setup_inputs(seed: int = 0) -> dict:
    key_list = jax.random.split(jax.random.key(seed), 10)
    nodes = jnp.clip(jax.random.uniform(key_list[0], (GROUPS, 3, NI, NJ), jnp.float32, -4.0, 4.0) * level_of(key_list[0], (GROUPS, 3, NI, NJ), ((0, 16), (2, 8)), -0.4, 0.0), -4.0, 4.0)
    panels = jnp.clip(jax.random.uniform(key_list[1], (GROUPS, 3, PANELS), jnp.float32, -4.0, 4.0) * level_of(key_list[1], (GROUPS, 3, PANELS), ((0, 16), (2, 8)), -0.4, 0.0), -4.0, 4.0)
    nu_field = jnp.clip(0.2 + 1.3 * jax.random.uniform(key_list[2], (GROUPS, NI, NJ), jnp.float32) ** level_of(key_list[2], (GROUPS, NI, NJ), ((0, 16), (1, 8)), -0.2, 0.2), 0.2, 1.5)
    vorticity = jnp.clip(jnp.exp(math.log(100.0) - 4.6051702 * jax.random.uniform(key_list[3], (GROUPS, NI, NJ), jnp.float32) ** level_of(key_list[3], (GROUPS, NI, NJ), ((0, 16), (1, 8)), -0.2, 0.2)), 1.0, 100.0)
    flow = gaussian(key_list[4], (GROUPS, 4, NI, NJ), 1.0, 6.0, ((0, 16), (2, 8)), jnp.float32)
    fringe_block = with_ends(jax.random.randint(key_list[5], (FR_ALL,), 0, NB_DEV), jax.random.fold_in(key_list[5], 1), 0, NB_DEV - 1).astype(jnp.int32)
    fringe_size = with_ends(jax.random.randint(key_list[6], (FR_ALL,), 1, 129), jax.random.fold_in(key_list[6], 1), 1, 128).astype(jnp.int32)
    fringe_owner_keys = jax.random.split(jax.random.fold_in(key_list[7], 1), FR_ALL // FR_DEV)
    fringe_owner_turns = jax.random.permutation(jax.random.fold_in(key_list[7], 3), FR_ALL // FR_DEV)
    fringe_owner = jax.vmap(lambda own, number: routed_block(jax.random.fold_in(key_list[7], 2), own, number, FR_DEV, DEVICES, 1, CAP, 2))(fringe_owner_keys, fringe_owner_turns).reshape((FR_ALL, 1))
    fringe_cell = with_ends(jax.random.randint(key_list[8], (FR_ALL,), 0, OB), jax.random.fold_in(key_list[8], 1), 0, OB - 1).astype(jnp.int32)
    return {"nodes": nodes, "panels": panels, "nu_field": nu_field, "vorticity": vorticity, "flow": flow, "fringe_block": fringe_block, "fringe_size": fringe_size, "fringe_owner": fringe_owner, "fringe_cell": fringe_cell}


def sa_step(nu_ext, dist, vort):
    centre = nu_ext[1:-1]
    east = nu_ext[2:]
    west = nu_ext[:-2]
    padded = jnp.pad(centre, ((0, 0), (1, 1)))
    north = padded[:, 2:]
    south = padded[:, :-2]
    flux = (1.0 + 0.5 * (centre + east)) * (east - centre) - (1.0 + 0.5 * (centre + west)) * (centre - west)
    flux = flux + (1.0 + 0.5 * (centre + north)) * (north - centre) - (1.0 + 0.5 * (centre + south)) * (centre - south)
    grads = 0.25 * ((east - west) * (east - west) + (north - south) * (north - south))
    diffusion = (flux + 0.622 * grads) / (2.0 / 3.0)
    ratio = centre / dist
    return centre + 0.02 * (0.1355 * vort * centre - 3.24 * ratio * ratio + diffusion)

def group_least(nodes_group, panels_group):
    points = nodes_group.reshape(3, -1)
    blocks = jnp.transpose(panels_group.reshape(3, N_BLK, PANELS_DEV), (1, 0, 2))

    def visit(best, panel_block):
        delta0 = points[0][:, None] - panel_block[0][None, :]
        delta1 = points[1][:, None] - panel_block[1][None, :]
        delta2 = points[2][:, None] - panel_block[2][None, :]
        dsq = delta0 * delta0 + delta1 * delta1 + delta2 * delta2
        return (jnp.minimum(best, lax.optimization_barrier(jnp.min(dsq, axis=1))), None)
    init = jnp.full((points.shape[1],), 1e+30, jnp.float32)
    best, unused = lax.scan(visit, init, blocks)
    return best.reshape(NI, NJ)

def reference(nodes, panels, nu_field, vorticity, flow, fringe_block, fringe_size, fringe_owner, fringe_cell):
    least = lax.map(lambda pair: group_least(pair[0], pair[1]), (nodes, panels))
    wall_distance = jnp.sqrt(least + 0.25)

    def advance(args):
        nu_now, dist, vort = args
        for step in range(2):
            ext = jnp.concatenate([nu_now[-1:], nu_now, nu_now[:1]], axis=0)
            nu_now = sa_step(ext, dist, vort)
        return nu_now
    nu_next = lax.map(advance, (nu_field, wall_distance, vorticity))
    state = jnp.concatenate([nu_next[:, None], flow], axis=1)
    jblocks = NJ // 128
    state = state.reshape(GROUPS, VARS, NI * jblocks, BLOCK)
    slots = jnp.arange(FR_ALL, dtype=jnp.int32)
    device = slots // FR_DEV
    group = device // N_BLK
    local = device % N_BLK
    row = local * NB_DEV + fringe_block
    values = state[group, :, row, :]
    live = (jnp.arange(BLOCK, dtype=jnp.int32)[None, :] < fringe_size[:, None]).astype(jnp.float32)
    values = values * live[:, None, :]
    target = fringe_owner[:, 0] * OB + fringe_cell
    offbody = jnp.zeros((OB_ALL, VARS, BLOCK), jnp.float32).at[target].add(values)
    return (wall_distance, nu_next, offbody)
```

```python
import functools

import jax
import jax.numpy as jnp
from jax import lax
from jax.experimental import pallas as pl
from jax.experimental.pallas import tpu as pltpu
from jax.sharding import PartitionSpec as P

BLOCK = 128
VARS = 5
CAP = 2
OB = 16
PEERS = 8
DEVS = 128
LINES = 16
NJ = 256
PQ = 4
PAY = 40
NU0 = 16
VO0 = 24
ND0 = 28
FR = 9
F32 = jnp.float32
BF16 = jnp.bfloat16


def iota(shape, axis):
    return lax.broadcasted_iota(jnp.int32, shape, axis)


def split3(v):
    high = v.astype(BF16)
    rest = v - high.astype(F32)
    mid = rest.astype(BF16)
    low = (rest - mid.astype(F32)).astype(BF16)
    return high, mid, low


def onehot(cond):
    return jnp.where(cond, 1.0, 0.0).astype(BF16)


def contract_lanes(a, b):
    return lax.dot_general(a, b, (((1,), (1,)), ((), ())), preferred_element_type=F32)


def halves(rows):
    return jnp.concatenate([rows[:, :BLOCK], rows[:, BLOCK:]], axis=0)


def pack_kernel(nodes_ref, panels_ref, nu_ref, vort_ref, out_ref):
    def put(row, value):
        out_ref[pl.ds(row, 1), :] = value

    p = [panels_ref[c] for c in range(3)]
    square = p[0] * p[0] + p[1] * p[1] + p[2] * p[2]
    for q in range(PQ):
        for c, vec in enumerate((p[0], p[1], p[2], square)):
            put(q * 4 + c, vec[:, q * BLOCK : (q + 1) * BLOCK])
    for half in range(2):
        lanes = slice(half * BLOCK, (half + 1) * BLOCK)
        for at, line in enumerate((0, 1, LINES - 2, LINES - 1)):
            put(NU0 + at * 2 + half, nu_ref[line : line + 1, lanes])
        for at, line in enumerate((0, LINES - 1)):
            put(VO0 + at * 2 + half, vort_ref[line : line + 1, lanes])
            for c in range(3):
                put(ND0 + c * 4 + at * 2 + half, nodes_ref[c, line : line + 1, lanes])
    block = out_ref[0:PAY, :]
    for s in range(1, PEERS):
        out_ref[s * PAY : (s + 1) * PAY, :] = block


def route_kernel(owner_ref, block_ref, size_ref, cell_ref, flow_ref, send_ref, pick_ref, live_ref):
    square = (DEVS, DEVS)
    row = iota(square, 0)
    lane = iota(square, 1)
    owner = owner_ref[...]
    hits = onehot(jnp.broadcast_to(owner, square) == row)
    before = onehot(row < lane)
    earlier = jnp.dot(hits, before, preferred_element_type=F32)
    rank = jnp.sum(hits.astype(F32) * earlier, axis=0, keepdims=True)
    slot = owner * CAP + rank.astype(jnp.int32)
    block = block_ref[...]
    place = (block % 2) * LINES + block // 2
    places = onehot((jnp.broadcast_to(place, square) == row % 32) & (row < 96))
    sizes = jnp.broadcast_to(size_ref[...], square).astype(F32).astype(BF16)
    cell = jnp.broadcast_to(cell_ref[...], square)
    state = jnp.concatenate([halves(flow_ref[v]) for v in range(VARS - 1)], axis=1)
    high, mid, low = split3(state)
    table = jnp.concatenate([high, mid, low, jnp.zeros_like(high)], axis=0)
    cells = None
    for r in range(CAP):
        sel = onehot(jnp.broadcast_to(slot, square) == row * CAP + r)
        pick = contract_lanes(sel, places)
        live = jnp.where(lane.astype(F32) < contract_lanes(sel, sizes), 1.0, 0.0)
        named = contract_lanes(sel, onehot((cell == row - r * OB) & (row < (r + 1) * OB)))
        cells = named if cells is None else cells + named
        pick_ref[pl.ds(r, DEVS, stride=CAP), :] = pick
        live_ref[pl.ds(r, DEVS, stride=CAP), :] = live
        values = jnp.dot(pick.astype(BF16), table, preferred_element_type=F32)
        for v in range(VARS - 1):
            send_ref[pl.ds(r * (VARS - 1) + v, DEVS, stride=FR), :] = (
                values[:, v * BLOCK : (v + 1) * BLOCK] * live
            )
    send_ref[pl.ds(FR - 1, DEVS, stride=FR), :] = cells


def sa_step(centre, east, west, dist, vort):
    lane = iota(centre.shape, 1)
    north = jnp.where(lane == NJ - 1, 0.0, pltpu.roll(centre, NJ - 1, 1))
    south = jnp.where(lane == 0, 0.0, pltpu.roll(centre, 1, 1))
    flux = (1.0 + 0.5 * (centre + east)) * (east - centre) - (1.0 + 0.5 * (centre + west)) * (
        centre - west
    )
    flux = (
        flux
        + (1.0 + 0.5 * (centre + north)) * (north - centre)
        - (1.0 + 0.5 * (centre + south)) * (centre - south)
    )
    grads = 0.25 * ((east - west) * (east - west) + (north - south) * (north - south))
    diffusion = (flux + 0.622 * grads) * 1.5
    ratio = centre / dist
    return centre + 0.02 * (0.1355 * vort * centre - 3.24 * ratio * ratio + diffusion)


def step_kernel(
    got_ref, nodes_ref, nu_ref, vort_ref, pick_ref, live_ref,
    dist_ref, next_ref, send_ref,
    lhs_ref, node_ext, nu_ext, vort_ext, dist_ext,
):
    me = lax.axis_index("blk")
    left = lax.rem(me + PEERS - 1, PEERS) * PAY
    right = lax.rem(me + 1, PEERS) * PAY

    def edge(base, row):
        return jnp.concatenate(
            [got_ref[pl.ds(base + row, 1), :], got_ref[pl.ds(base + row + 1, 1), :]], axis=1
        )

    for c in range(3):
        node_ext[c, 1 : 1 + LINES, :] = nodes_ref[c]
        node_ext[c, 0:1, :] = edge(left, ND0 + c * 4 + 2)
        node_ext[c, 1 + LINES : 2 + LINES, :] = edge(right, ND0 + c * 4)
    nu_ext[2 : 2 + LINES, :] = nu_ref[...]
    vort_ext[1 : 1 + LINES, :] = vort_ref[...]
    for at in range(2):
        nu_ext[at : at + 1, :] = edge(left, NU0 + 4 + at * 2)
        nu_ext[2 + LINES + at : 3 + LINES + at, :] = edge(right, NU0 + at * 2)
    vort_ext[0:1, :] = edge(left, VO0 + 2)
    vort_ext[1 + LINES : 2 + LINES, :] = edge(right, VO0)

    for s in range(PEERS):
        high, mid, low = [t.astype(F32) for t in split3(got_ref[pl.ds(s * PAY, PQ * 4), :])]
        none = jnp.zeros_like(high)
        terms = jnp.concatenate([high, high, high, mid, mid, low, none, none], axis=0)
        lhs_ref[s * BLOCK : (s + 1) * BLOCK, :] = terms.T.astype(BF16)

    c4 = iota((PQ * 4, NJ), 0) % 4
    q4 = iota((PQ * 4, NJ), 0) // 4

    def line(i, unused):
        x, y, z = [
            jnp.broadcast_to(node_ext[c, pl.ds(i, 1), :], (PQ * 4, NJ)) for c in range(3)
        ]
        square = (x * x + y * y + z * z)[0:1]
        base = jnp.where(c4 == 0, x, jnp.where(c4 == 1, y, z)) * -2.0
        base = jnp.where(c4 == 3, 1.0, base)
        best = None
        for q in range(PQ):
            high, mid, low = split3(jnp.where(q4 == q, base, 0.0))
            none = jnp.zeros_like(high)
            w = jnp.concatenate([high, mid, low, high, mid, high, none, none], axis=0)
            rest = jnp.dot(lhs_ref[...], w, preferred_element_type=F32)
            low8 = jnp.min(rest.reshape(PEERS * BLOCK // 8, 8, NJ), axis=0)
            best = low8 if best is None else jnp.minimum(best, low8)
        least = jnp.min(best, axis=0, keepdims=True) + square
        dist_ext[pl.ds(i, 1), :] = jnp.sqrt(jnp.maximum(least, 0.0) + 0.25)
        return unused

    lax.fori_loop(0, LINES + 2, line, 0)

    mid_nu = sa_step(
        nu_ext[1 : 3 + LINES, :],
        nu_ext[2 : 4 + LINES, :],
        nu_ext[0 : 2 + LINES, :],
        dist_ext[0 : 2 + LINES, :],
        vort_ext[0 : 2 + LINES, :],
    )
    nu_ext[0 : 2 + LINES, :] = mid_nu
    dist = dist_ext[1 : 1 + LINES, :]
    new = sa_step(
        nu_ext[1 : 1 + LINES, :],
        nu_ext[2 : 2 + LINES, :],
        nu_ext[0:LINES, :],
        dist,
        vort_ref[...],
    )
    dist_ref[...] = dist
    next_ref[...] = new
    high, mid, low = split3(halves(new))
    table = jnp.concatenate([high, mid, low, jnp.zeros_like(high)], axis=0)
    values = jnp.dot(pick_ref[...].astype(BF16), table, preferred_element_type=F32)
    send_ref[...] = values * live_ref[...]


def add_up(chosen, rows):
    total = None
    for part in split3(rows):
        term = jnp.dot(chosen, part, preferred_element_type=F32)
        total = term if total is None else total + term
    return total


def flow_sum_kernel(got_ref, sums_ref, chosen_ref):
    cells = got_ref[pl.ds(FR - 1, DEVS, stride=FR), :].T
    chosen = jnp.concatenate([cells[r * OB : (r + 1) * OB] for r in range(CAP)], axis=1)
    chosen_ref[...] = chosen
    chosen = chosen.astype(BF16)
    for v in range(VARS - 1):
        rows = jnp.concatenate(
            [
                got_ref[pl.ds(r * (VARS - 1) + v, DEVS, stride=FR), :]
                for r in range(CAP)
            ],
            axis=0,
        )
        sums_ref[v] = add_up(chosen, rows)


def nu_sum_kernel(got_ref, sums_ref, chosen_ref, out_ref):
    rows = jnp.concatenate(
        [got_ref[pl.ds(r, DEVS, stride=CAP), :] for r in range(CAP)], axis=0
    )
    out_ref[0] = add_up(chosen_ref[...].astype(BF16), rows)
    out_ref[1:VARS] = sums_ref[...]


def call(kernel, outs, *args, scratch=()):
    return pl.pallas_call(
        kernel,
        out_shape=tuple(jax.ShapeDtypeStruct(shape, F32) for shape in outs),
        scratch_shapes=list(scratch),
    )(*args)


def exchange(rows, count, axes):
    sent = rows.reshape(count, 1, -1)
    got = lax.all_to_all(sent, axes, split_axis=0, concat_axis=0, tiled=True)
    return got.reshape(rows.shape)


def per_device(
    nodes, panels, nu_field, vorticity, flow, fringe_block, fringe_size, fringe_owner, fringe_cell
):
    nodes, nu, vort, flow = nodes[0], nu_field[0], vorticity[0], flow[0]
    (pay,) = call(
        pack_kernel, [(PEERS * PAY, BLOCK)], nodes, panels.reshape(3, 1, PQ * BLOCK), nu, vort
    )
    pay = exchange(pay, PEERS, "blk")
    wide = (1, DEVS)
    send, pick, live = call(
        route_kernel,
        [(DEVS * FR, BLOCK), (DEVS * CAP, BLOCK), (DEVS * CAP, BLOCK)],
        fringe_owner.reshape(wide),
        fringe_block.reshape(wide),
        fringe_size.reshape(wide),
        fringe_cell.reshape(wide),
        flow,
    )
    flow_rows = exchange(send, DEVS, ("grp", "blk"))
    line = (LINES, NJ)
    ext = pltpu.VMEM((24, NJ), F32)
    dist, nu_next, send = call(
        step_kernel,
        [line, line, (DEVS * CAP, BLOCK)],
        pay, nodes, nu, vort, pick, live,
        scratch=(
            pltpu.VMEM((PEERS * BLOCK, BLOCK), BF16),
            pltpu.VMEM((3, 24, NJ), F32),
            ext, ext, ext,
        ),
    )
    nu_rows = exchange(send, DEVS, ("grp", "blk"))
    sums, chosen = call(
        flow_sum_kernel, [(VARS - 1, OB, BLOCK), (OB, CAP * DEVS)], flow_rows
    )
    (offbody,) = call(nu_sum_kernel, [(VARS, OB, BLOCK)], nu_rows, sums, chosen)
    return (dist[None], nu_next[None], jnp.transpose(offbody, (1, 0, 2)))


def solution(mesh):
    in_specs = (
        P("grp", None, "blk", None),
        P("grp", None, "blk"),
        P("grp", "blk", None),
        P("grp", "blk", None),
        P("grp", None, "blk", None),
        P(("grp", "blk")),
        P(("grp", "blk")),
        P(("grp", "blk"), None),
        P(("grp", "blk")),
    )
    out_specs = (P("grp", "blk", None), P("grp", "blk", None), P(("grp", "blk"), None, None))
    return jax.shard_map(
        per_device, mesh=mesh, in_specs=in_specs, out_specs=out_specs, check_vma=False
    )
```

```python
import functools

import jax
import jax.numpy as jnp
from jax import lax
from jax.experimental import pallas as pl
from jax.experimental.pallas import tpu as pltpu
from jax.sharding import PartitionSpec as P

BLOCK = 128
VARS = 5
CAP = 2
OB = 16
PEERS = 8
DEVS = 128
LINES = 16
NJ = 256
PQ = 4
PAY = 24
PAN = 12
NU0 = 12
VO0 = 16
ND0 = 18
FR = 11
UNROLL = 8
OWN_UNROLL = 8
F32 = jnp.float32
BF16 = jnp.bfloat16


def iota(shape, axis):
    return lax.broadcasted_iota(jnp.int32, shape, axis)


def split3(v):
    high = v.astype(BF16)
    rest = v - high.astype(F32)
    mid = rest.astype(BF16)
    low = (rest - mid.astype(F32)).astype(BF16)
    return high, mid, low


def onehot(cond):
    return jnp.where(cond, 1.0, 0.0).astype(BF16)


def contract_lanes(a, b):
    return lax.dot_general(a, b, (((1,), (1,)), ((), ())), preferred_element_type=F32)


def halves(rows):
    return jnp.concatenate([rows[:, :BLOCK], rows[:, BLOCK:]], axis=0)


def pack_kernel(nodes_ref, panels_ref, nu_ref, vort_ref, out_ref):
    def fill(base, nu_line, line):
        def put(row, value):
            out_ref[pl.ds(base + row, 1), :] = value

        for c in range(3):
            vec = panels_ref[c]
            for q in range(PQ):
                put(c * PQ + q, vec[:, q * BLOCK : (q + 1) * BLOCK])
        for half in range(2):
            lanes = slice(half * BLOCK, (half + 1) * BLOCK)
            for at in range(2):
                put(NU0 + at * 2 + half, nu_ref[nu_line + at : nu_line + at + 1, lanes])
            put(VO0 + half, vort_ref[line : line + 1, lanes])
            for c in range(3):
                put(ND0 + c * 2 + half, nodes_ref[c, line : line + 1, lanes])

    fill(0, 0, 0)
    first = out_ref[0:PAY, :]
    for s in range(1, PEERS):
        out_ref[s * PAY : (s + 1) * PAY, :] = first
    after = lax.rem(lax.axis_index("blk") + 1, PEERS)
    fill(after * PAY, LINES - 2, LINES - 1)


def panel_terms(raw):
    square = raw[0:4] * raw[0:4] + raw[4:8] * raw[4:8] + raw[8:12] * raw[8:12]
    high, mid, low = [
        t.astype(F32) for t in split3(jnp.concatenate([raw, square], axis=0))
    ]
    none = jnp.zeros_like(high)
    terms = jnp.concatenate([high, high, high, mid, mid, low, none, none], axis=0)
    return terms.T.astype(BF16)


def line_least(coords, lhs):
    c4 = iota((PQ * 4, NJ), 0) // 4
    q4 = iota((PQ * 4, NJ), 0) % 4
    x, y, z = [jnp.broadcast_to(v, (PQ * 4, NJ)) for v in coords]
    base = jnp.where(c4 == 0, x, jnp.where(c4 == 1, y, z)) * -2.0
    base = jnp.where(c4 == 3, 1.0, base)
    best = None
    for q in range(PQ):
        high, mid, low = split3(jnp.where(q4 == q, base, 0.0))
        none = jnp.zeros_like(high)
        w = jnp.concatenate([high, mid, low, high, mid, high, none, none], axis=0)
        rest = jnp.dot(lhs, w, preferred_element_type=F32)
        least = jnp.min(rest.reshape(lhs.shape[0] // 8, 8, NJ), axis=0)
        best = least if best is None else jnp.minimum(best, least)
    return best


def own_kernel(panels_ref, nodes_ref, least_ref, raw_ref, lhs_ref):
    for c in range(3):
        vec = panels_ref[c]
        for q in range(PQ):
            raw_ref[c * PQ + q : c * PQ + q + 1, :] = vec[:, q * BLOCK : (q + 1) * BLOCK]
    lhs_ref[...] = panel_terms(raw_ref[0:PAN, :])

    def line(i, unused):
        best = line_least([nodes_ref[c, pl.ds(i, 1), :] for c in range(3)], lhs_ref[...])
        least_ref[pl.ds(i, 1), :] = jnp.min(best, axis=0, keepdims=True)
        return unused

    lax.fori_loop(0, LINES, line, 0, unroll=OWN_UNROLL)


def route_kernel(owner_ref, block_ref, size_ref, cell_ref, flow_ref, send_ref, pick_ref, live_ref):
    square = (DEVS, DEVS)
    row = iota(square, 0)
    lane = iota(square, 1)
    owner = owner_ref[...]
    hits = onehot(jnp.broadcast_to(owner, square) == row)
    before = onehot(row < lane)
    earlier = jnp.dot(hits, before, preferred_element_type=F32)
    rank = jnp.sum(hits.astype(F32) * earlier, axis=0, keepdims=True)
    slot = owner * CAP + rank.astype(jnp.int32)
    block = block_ref[...]
    place = (block % 2) * LINES + block // 2
    places = onehot((jnp.broadcast_to(place, square) == row % 32) & (row < 96))
    sizes = jnp.broadcast_to(size_ref[...], square).astype(F32).astype(BF16)
    cell = jnp.broadcast_to(cell_ref[...], square)
    state = jnp.concatenate([halves(flow_ref[v]) for v in range(VARS - 1)], axis=1)
    high, mid, low = split3(state)
    table = jnp.concatenate([high, mid, low, jnp.zeros_like(high)], axis=0)
    cells = None
    for r in range(CAP):
        sel = onehot(jnp.broadcast_to(slot, square) == row * CAP + r)
        pick = contract_lanes(sel, places)
        live = jnp.where(lane.astype(F32) < contract_lanes(sel, sizes), 1.0, 0.0)
        named = contract_lanes(sel, onehot((cell == row - r * OB) & (row < (r + 1) * OB)))
        cells = named if cells is None else cells + named
        pick_ref[pl.ds(r * DEVS, DEVS), :] = pick
        live_ref[pl.ds(r * DEVS, DEVS), :] = live
        values = jnp.dot(pick.astype(BF16), table, preferred_element_type=F32)
        for v in range(VARS - 1):
            send_ref[pl.ds(r * VARS + 1 + v, DEVS, stride=FR), :] = (
                values[:, v * BLOCK : (v + 1) * BLOCK] * live
            )
    send_ref[pl.ds(FR - 1, DEVS, stride=FR), :] = cells


def sa_step(centre, east, west, dist, vort):
    lane = iota(centre.shape, 1)
    north = jnp.where(lane == NJ - 1, 0.0, pltpu.roll(centre, NJ - 1, 1))
    south = jnp.where(lane == 0, 0.0, pltpu.roll(centre, 1, 1))
    flux = (1.0 + 0.5 * (centre + east)) * (east - centre) - (1.0 + 0.5 * (centre + west)) * (
        centre - west
    )
    flux = (
        flux
        + (1.0 + 0.5 * (centre + north)) * (north - centre)
        - (1.0 + 0.5 * (centre + south)) * (centre - south)
    )
    grads = 0.25 * ((east - west) * (east - west) + (north - south) * (north - south))
    diffusion = (flux + 0.622 * grads) * 1.5
    ratio = centre / dist
    return centre + 0.02 * (0.1355 * vort * centre - 3.24 * ratio * ratio + diffusion)


def step_kernel(
    got_ref, own_ref, nodes_ref, nu_ref, vort_ref, pick_ref, live_ref, rows_ref,
    dist_ref, next_ref, send_ref,
    lhs_ref, node_ext, nu_ext, vort_ext, dist_ext,
):
    me = lax.axis_index("blk")

    def member(k):
        return pl.multiple_of(lax.rem(me + k, PEERS) * PAY, 8)

    left, right = member(PEERS - 1), member(1)

    def edge(base, row):
        return jnp.concatenate(
            [got_ref[pl.ds(base + row, 1), :], got_ref[pl.ds(base + row + 1, 1), :]], axis=1
        )

    for c in range(3):
        node_ext[c, 1 : 1 + LINES, :] = nodes_ref[c]
        node_ext[c, 0:1, :] = edge(left, ND0 + c * 2)
        node_ext[c, 1 + LINES : 2 + LINES, :] = edge(right, ND0 + c * 2)
    nu_ext[2 : 2 + LINES, :] = nu_ref[...]
    vort_ext[1 : 1 + LINES, :] = vort_ref[...]
    for at in range(2):
        nu_ext[at : at + 1, :] = edge(left, NU0 + at * 2)
        nu_ext[2 + LINES + at : 3 + LINES + at, :] = edge(right, NU0 + at * 2)
    vort_ext[0:1, :] = edge(left, VO0)
    vort_ext[1 + LINES : 2 + LINES, :] = edge(right, VO0)

    for k in range(PEERS):
        raw = got_ref[pl.ds(member(k + 1), PAN), :]
        lhs_ref[k * BLOCK : (k + 1) * BLOCK, :] = panel_terms(raw)

    def finish(i, least):
        x, y, z = [node_ext[c, pl.ds(i, 1), :] for c in range(3)]
        least = jnp.maximum(least + (x * x + y * y + z * z), 0.0)
        dist_ext[pl.ds(i, 1), :] = jnp.sqrt(least + 0.25)

    def coords(i):
        return [node_ext[c, pl.ds(i, 1), :] for c in range(3)]

    def line(i, unused):
        best = line_least(coords(i), lhs_ref[0 : (PEERS - 1) * BLOCK, :])
        best = jnp.minimum(jnp.min(best, axis=0, keepdims=True), own_ref[pl.ds(i - 1, 1), :])
        finish(i, best)
        return unused

    for i in (0, 1 + LINES):
        finish(i, jnp.min(line_least(coords(i), lhs_ref[...]), axis=0, keepdims=True))
    lax.fori_loop(1, 1 + LINES, line, 0, unroll=UNROLL)

    mid_nu = sa_step(
        nu_ext[1 : 3 + LINES, :],
        nu_ext[2 : 4 + LINES, :],
        nu_ext[0 : 2 + LINES, :],
        dist_ext[0 : 2 + LINES, :],
        vort_ext[0 : 2 + LINES, :],
    )
    nu_ext[0 : 2 + LINES, :] = mid_nu
    dist = dist_ext[1 : 1 + LINES, :]
    new = sa_step(
        nu_ext[1 : 1 + LINES, :],
        nu_ext[2 : 2 + LINES, :],
        nu_ext[0:LINES, :],
        dist,
        vort_ref[...],
    )
    dist_ref[...] = dist
    next_ref[...] = new
    high, mid, low = split3(halves(new))
    table = jnp.concatenate([high, mid, low, jnp.zeros_like(high)], axis=0)
    values = jnp.dot(pick_ref[...].astype(BF16), table, preferred_element_type=F32)
    values = values * live_ref[...]
    for r in range(CAP):
        send_ref[pl.ds(r * VARS, DEVS, stride=FR), :] = values[r * DEVS : (r + 1) * DEVS]


def add_up(chosen, rows):
    total = None
    for part in split3(rows):
        term = jnp.dot(chosen, part, preferred_element_type=F32)
        total = term if total is None else total + term
    return total


def sum_kernel(got_ref, out_ref):
    cells = got_ref[pl.ds(FR - 1, DEVS, stride=FR), :].T
    chosen = jnp.concatenate([cells[r * OB : (r + 1) * OB] for r in range(CAP)], axis=1)
    chosen = chosen.astype(BF16)
    for v in range(VARS):
        rows = jnp.concatenate(
            [got_ref[pl.ds(r * VARS + v, DEVS, stride=FR), :] for r in range(CAP)], axis=0
        )
        out_ref[v] = add_up(chosen, rows)


def call(kernel, outs, *args, scratch=(), alias=(), hbm=(), fetch=True):
    if fetch:
        args = [pltpu.with_memory_space_constraint(a, pltpu.VMEM) for a in args]
    vmem = pl.BlockSpec(memory_space=pltpu.VMEM)
    return pl.pallas_call(
        kernel,
        out_shape=tuple(
            (jax.ShapeDtypeStruct if n in hbm else pltpu.VMEM)(shape, F32)
            for n, shape in enumerate(outs)
        ),
        in_specs=[vmem] * len(args),
        out_specs=tuple(vmem for shape in outs),
        scratch_shapes=list(scratch),
        input_output_aliases=dict(alias),
    )(*args)


def exchange(rows, count, axes):
    sent = rows.reshape(count, 1, -1)
    got = lax.all_to_all(sent, axes, split_axis=0, concat_axis=0, tiled=True)
    return got.reshape(rows.shape)


def per_device(
    nodes, panels, nu_field, vorticity, flow, fringe_block, fringe_size, fringe_owner, fringe_cell
):
    nodes, nu, vort, flow = nodes[0], nu_field[0], vorticity[0], flow[0]
    flat = panels.reshape(3, 1, PQ * BLOCK)
    (pay,) = call(
        pack_kernel, [(PEERS * PAY, BLOCK)], nodes, flat, nu, vort, fetch=False
    )
    pay = exchange(pay, PEERS, "blk")
    (own,) = call(
        own_kernel,
        [(LINES, NJ)],
        flat,
        nodes,
        scratch=(pltpu.VMEM((16, BLOCK), F32), pltpu.VMEM((BLOCK, BLOCK), BF16)),
    )
    wide = (1, DEVS)
    send, pick, live = call(
        route_kernel,
        [(DEVS * FR, BLOCK), (DEVS * CAP, BLOCK), (DEVS * CAP, BLOCK)],
        fringe_owner.reshape(wide),
        fringe_block.reshape(wide),
        fringe_size.reshape(wide),
        fringe_cell.reshape(wide),
        flow,
    )
    line = (LINES, NJ)
    ext = pltpu.VMEM((24, NJ), F32)
    dist, nu_next, send = call(
        step_kernel,
        [line, line, (DEVS * FR, BLOCK)],
        pay, own, nodes, nu, vort, pick, live, send,
        scratch=(
            pltpu.VMEM((PEERS * BLOCK, BLOCK), BF16),
            pltpu.VMEM((3, 24, NJ), F32),
            ext, ext, ext,
        ),
        alias=((7, 2),),
        hbm=(0, 1),
    )
    got = exchange(send, DEVS, ("grp", "blk"))
    (offbody,) = call(sum_kernel, [(VARS, OB, BLOCK)], got, hbm=(0,))
    return (dist[None], nu_next[None], jnp.transpose(offbody, (1, 0, 2)))


def solution(mesh):
    in_specs = (
        P("grp", None, "blk", None),
        P("grp", None, "blk"),
        P("grp", "blk", None),
        P("grp", "blk", None),
        P("grp", None, "blk", None),
        P(("grp", "blk")),
        P(("grp", "blk")),
        P(("grp", "blk"), None),
        P(("grp", "blk")),
    )
    out_specs = (P("grp", "blk", None), P("grp", "blk", None), P(("grp", "blk"), None, None))
    return jax.shard_map(
        per_device, mesh=mesh, in_specs=in_specs, out_specs=out_specs, check_vma=False
    )
```

```python
import functools

import jax
import jax.numpy as jnp
from jax import lax
from jax.experimental import pallas as pl
from jax.experimental.pallas import tpu as pltpu
from jax.sharding import PartitionSpec as P

BLOCK = 128
VARS = 5
CAP = 2
OB = 16
PEERS = 8
DEVS = 128
LINES = 16
NJ = 256
PQ = 4
PAN = 12
EDGE = 12
PAY = 40
NEAR = 36
FR = 11
UNROLL = 16
OWN_UNROLL = 16
FLIP = 69
F32 = jnp.float32
BF16 = jnp.bfloat16


def iota(shape, axis):
    return lax.broadcasted_iota(jnp.int32, shape, axis)


def split3(v):
    high = v.astype(BF16)
    rest = v - high.astype(F32)
    mid = rest.astype(BF16)
    low = (rest - mid.astype(F32)).astype(BF16)
    return high, mid, low


def onehot(cond):
    return jnp.where(cond, 1.0, 0.0).astype(BF16)


def contract_lanes(a, b):
    return lax.dot_general(a, b, (((1,), (1,)), ((), ())), preferred_element_type=F32)


def halves(rows):
    return jnp.concatenate([rows[:, :BLOCK], rows[:, BLOCK:]], axis=0)


def pack_kernel(nodes_ref, panels_ref, nu_ref, vort_ref, out_ref):
    def put(row, value):
        out_ref[pl.ds(row, 1), :] = value

    for c in range(3):
        vec = panels_ref[c]
        for q in range(PQ):
            put(c * PQ + q, vec[:, q * BLOCK : (q + 1) * BLOCK])
    odd = lax.rem(lax.axis_index("blk"), 2)
    for base, nu_line, line in (
        (PAN + EDGE * (1 - odd), 0, 0),
        (PAN + EDGE * odd, LINES - 2, LINES - 1),
    ):
        for half in range(2):
            lanes = slice(half * BLOCK, (half + 1) * BLOCK)
            for at in range(2):
                put(base + at * 2 + half, nu_ref[nu_line + at : nu_line + at + 1, lanes])
            put(base + 4 + half, vort_ref[line : line + 1, lanes])
            for c in range(3):
                put(base + 6 + c * 2 + half, nodes_ref[c, line : line + 1, lanes])
    out_ref[PAN + 2 * EDGE :, :] = jnp.zeros((PAY - PAN - 2 * EDGE, BLOCK), F32)


def join_kernel(pay_ref, mate_ref, least_ref, near_ref):
    near_ref[0:PAN, :] = pay_ref[0:PAN, :]
    near_ref[PAN : 2 * PAN, :] = mate_ref[0:PAN, :]
    near_ref[2 * PAN : NEAR, :] = mate_ref[PAN + EDGE : PAN + 2 * EDGE, :]


def panel_terms(raw):
    square = raw[0:4] * raw[0:4] + raw[4:8] * raw[4:8] + raw[8:12] * raw[8:12]
    high, mid, low = [
        t.astype(F32) for t in split3(jnp.concatenate([raw, square], axis=0))
    ]
    none = jnp.zeros_like(high)
    terms = jnp.concatenate([high, high, high, mid, mid, low, none, none], axis=0)
    return terms.T.astype(BF16)


def line_least(coords, lhs):
    c4 = iota((PQ * 4, NJ), 0) // 4
    q4 = iota((PQ * 4, NJ), 0) % 4
    x, y, z = [jnp.broadcast_to(v, (PQ * 4, NJ)) for v in coords]
    base = jnp.where(c4 == 0, x, jnp.where(c4 == 1, y, z)) * -2.0
    base = jnp.where(c4 == 3, 1.0, base)
    best = None
    for q in range(PQ):
        high, mid, low = split3(jnp.where(q4 == q, base, 0.0))
        none = jnp.zeros_like(high)
        w = jnp.concatenate([high, mid, low, high, mid, high, none, none], axis=0)
        rest = jnp.dot(lhs, w, preferred_element_type=F32)
        least = jnp.min(rest.reshape(lhs.shape[0] // 8, 8, NJ), axis=0)
        best = least if best is None else jnp.minimum(best, least)
    return best


def lines_least(nodes_ref, lhs_ref, least_ref, before):
    def line(i, unused):
        best = line_least([nodes_ref[c, pl.ds(i, 1), :] for c in range(3)], lhs_ref[...])
        best = jnp.min(best, axis=0, keepdims=True)
        if before is not None:
            best = jnp.minimum(best, before[pl.ds(i, 1), :])
        least_ref[pl.ds(i, 1), :] = best
        return unused

    lax.fori_loop(0, LINES, line, 0, unroll=OWN_UNROLL)


def own_least(panels_ref, nodes_ref, least_ref, raw_ref, lhs_ref):
    for c in range(3):
        vec = panels_ref[c]
        for q in range(PQ):
            raw_ref[c * PQ + q : c * PQ + q + 1, :] = vec[:, q * BLOCK : (q + 1) * BLOCK]
    lhs_ref[...] = panel_terms(raw_ref[0:PAN, :])
    lines_least(nodes_ref, lhs_ref, least_ref, None)


def mate_kernel(mate_ref, nodes_ref, own_ref, least_ref, lhs_ref):
    lhs_ref[...] = panel_terms(mate_ref[0:PAN, :])
    lines_least(nodes_ref, lhs_ref, least_ref, own_ref)


def early_kernel(
    panels_ref, nodes_ref, owner_ref, block_ref, size_ref, cell_ref, flow_ref,
    least_ref, send_ref, pick_ref, live_ref,
    raw_ref, lhs_ref,
):
    own_least(panels_ref, nodes_ref, least_ref, raw_ref, lhs_ref)
    square = (DEVS, DEVS)
    row = iota(square, 0)
    lane = iota(square, 1)
    owner = owner_ref[...]
    hits = onehot(jnp.broadcast_to(owner, square) == row)
    before = onehot(row < lane)
    earlier = jnp.dot(hits, before, preferred_element_type=F32)
    rank = jnp.sum(hits.astype(F32) * earlier, axis=0, keepdims=True)
    slot = (owner ^ FLIP) * CAP + rank.astype(jnp.int32)
    block = block_ref[...]
    place = (block % 2) * LINES + block // 2
    places = onehot((jnp.broadcast_to(place, square) == row % 32) & (row < 96))
    sizes = jnp.broadcast_to(size_ref[...], square).astype(F32).astype(BF16)
    cell = jnp.broadcast_to(cell_ref[...], square)
    state = jnp.concatenate([halves(flow_ref[v]) for v in range(VARS - 1)], axis=1)
    high, mid, low = split3(state)
    table = jnp.concatenate([high, mid, low, jnp.zeros_like(high)], axis=0)
    cells = None
    for r in range(CAP):
        sel = onehot(jnp.broadcast_to(slot, square) == row * CAP + r)
        pick = contract_lanes(sel, places)
        live = jnp.where(lane.astype(F32) < contract_lanes(sel, sizes), 1.0, 0.0)
        named = contract_lanes(sel, onehot((cell == row - r * OB) & (row < (r + 1) * OB)))
        cells = named if cells is None else cells + named
        pick_ref[pl.ds(r * DEVS, DEVS), :] = pick
        live_ref[pl.ds(r * DEVS, DEVS), :] = live
        values = jnp.dot(pick.astype(BF16), table, preferred_element_type=F32)
        for v in range(VARS - 1):
            send_ref[pl.ds(r * VARS + 1 + v, DEVS, stride=FR), :] = (
                values[:, v * BLOCK : (v + 1) * BLOCK] * live
            )
    send_ref[pl.ds(FR - 1, DEVS, stride=FR), :] = cells


def sa_step(centre, east, west, dist, vort):
    lane = iota(centre.shape, 1)
    north = jnp.where(lane == NJ - 1, 0.0, pltpu.roll(centre, NJ - 1, 1))
    south = jnp.where(lane == 0, 0.0, pltpu.roll(centre, 1, 1))
    flux = (1.0 + 0.5 * (centre + east)) * (east - centre) - (1.0 + 0.5 * (centre + west)) * (
        centre - west
    )
    flux = (
        flux
        + (1.0 + 0.5 * (centre + north)) * (north - centre)
        - (1.0 + 0.5 * (centre + south)) * (centre - south)
    )
    grads = 0.25 * ((east - west) * (east - west) + (north - south) * (north - south))
    diffusion = (flux + 0.622 * grads) * 1.5
    ratio = centre / dist
    return centre + 0.02 * (0.1355 * vort * centre - 3.24 * ratio * ratio + diffusion)


def step_kernel(
    pay_ref, mate_ref, three_ref, one_ref, two_ref, done_ref, nodes_ref, nu_ref, vort_ref, pick_ref, live_ref, rows_ref,
    dist_ref, next_ref, send_ref,
    lhs_ref, node_ext, nu_ext, vort_ext, dist_ext,
):
    me = lax.axis_index("blk")
    even = lax.rem(me, 2) == 0
    outer_in_one = lax.rem(me + me // 2, 2) == 1

    def edge(left, row):
        def lines(ref, at):
            return jnp.concatenate([ref[at : at + 1, :], ref[at + 1 : at + 2, :]], axis=1)

        outer = jnp.where(
            outer_in_one, lines(one_ref, 2 * PAN + row), lines(three_ref, 2 * PAN + row)
        )
        inner = lines(mate_ref, PAN + row)
        return jnp.where(even, outer, inner) if left else jnp.where(even, inner, outer)

    for c in range(3):
        node_ext[c, 1 : 1 + LINES, :] = nodes_ref[c]
        node_ext[c, 0:1, :] = edge(True, 6 + c * 2)
        node_ext[c, 1 + LINES : 2 + LINES, :] = edge(False, 6 + c * 2)
    nu_ext[2 : 2 + LINES, :] = nu_ref[...]
    vort_ext[1 : 1 + LINES, :] = vort_ref[...]
    for at in range(2):
        nu_ext[at : at + 1, :] = edge(True, at * 2)
        nu_ext[2 + LINES + at : 3 + LINES + at, :] = edge(False, at * 2)
    vort_ext[0:1, :] = edge(True, 4)
    vort_ext[1 + LINES : 2 + LINES, :] = edge(False, 4)

    sources = [(ref, at) for ref in (one_ref, two_ref, three_ref) for at in (0, PAN)]
    sources += [(pay_ref, 0), (mate_ref, 0)]
    for k, (ref, at) in enumerate(sources):
        lhs_ref[k * BLOCK : (k + 1) * BLOCK, :] = panel_terms(ref[at : at + PAN, :])

    def finish(i, least):
        x, y, z = [node_ext[c, pl.ds(i, 1), :] for c in range(3)]
        least = jnp.maximum(least + (x * x + y * y + z * z), 0.0)
        dist_ext[pl.ds(i, 1), :] = jnp.sqrt(least + 0.25)

    def coords(i):
        return [node_ext[c, pl.ds(i, 1), :] for c in range(3)]

    def line(i, unused):
        best = line_least(coords(i), lhs_ref[0 : (PEERS - 2) * BLOCK, :])
        best = jnp.minimum(jnp.min(best, axis=0, keepdims=True), done_ref[pl.ds(i - 1, 1), :])
        finish(i, best)
        return unused

    for i in (0, 1 + LINES):
        finish(i, jnp.min(line_least(coords(i), lhs_ref[...]), axis=0, keepdims=True))
    lax.fori_loop(1, 1 + LINES, line, 0, unroll=UNROLL)

    mid_nu = sa_step(
        nu_ext[1 : 3 + LINES, :],
        nu_ext[2 : 4 + LINES, :],
        nu_ext[0 : 2 + LINES, :],
        dist_ext[0 : 2 + LINES, :],
        vort_ext[0 : 2 + LINES, :],
    )
    nu_ext[0 : 2 + LINES, :] = mid_nu
    dist = dist_ext[1 : 1 + LINES, :]
    new = sa_step(
        nu_ext[1 : 1 + LINES, :],
        nu_ext[2 : 2 + LINES, :],
        nu_ext[0:LINES, :],
        dist,
        vort_ref[...],
    )
    dist_ref[...] = dist
    next_ref[...] = new
    high, mid, low = split3(halves(new))
    table = jnp.concatenate([high, mid, low, jnp.zeros_like(high)], axis=0)
    values = jnp.dot(pick_ref[...].astype(BF16), table, preferred_element_type=F32)
    values = values * live_ref[...]
    for r in range(CAP):
        send_ref[pl.ds(r * VARS, DEVS, stride=FR), :] = values[r * DEVS : (r + 1) * DEVS]


def add_up(chosen, rows):
    total = None
    for part in split3(rows):
        term = jnp.dot(chosen, part, preferred_element_type=F32)
        total = term if total is None else total + term
    return total


def sum_kernel(got_ref, out_ref):
    cells = got_ref[pl.ds(FR - 1, DEVS, stride=FR), :].T
    chosen = jnp.concatenate([cells[r * OB : (r + 1) * OB] for r in range(CAP)], axis=1)
    chosen = chosen.astype(BF16)
    for v in range(VARS):
        rows = jnp.concatenate(
            [got_ref[pl.ds(r * VARS + v, DEVS, stride=FR), :] for r in range(CAP)], axis=0
        )
        out_ref[v] = add_up(chosen, rows)


def call(kernel, outs, *args, scratch=(), alias=(), hbm=(), fetch=True):
    if fetch:
        args = [pltpu.with_memory_space_constraint(a, pltpu.VMEM) for a in args]
    vmem = pl.BlockSpec(memory_space=pltpu.VMEM)
    return pl.pallas_call(
        kernel,
        out_shape=tuple(
            (jax.ShapeDtypeStruct if n in hbm else pltpu.VMEM)(shape, F32)
            for n, shape in enumerate(outs)
        ),
        in_specs=[vmem] * len(args),
        out_specs=tuple(vmem for shape in outs),
        scratch_shapes=list(scratch),
        input_output_aliases=dict(alias),
    )(*args)


def exchange(rows, count, axes, groups=None):
    sent = rows.reshape(count, 1, -1)
    got = lax.all_to_all(sent, axes, split_axis=0, concat_axis=0, tiled=True, axis_index_groups=groups)
    return got.reshape(rows.shape)


def per_device(
    nodes, panels, nu_field, vorticity, flow, fringe_block, fringe_size, fringe_owner, fringe_cell
):
    nodes, nu, vort, flow = nodes[0], nu_field[0], vorticity[0], flow[0]
    flat = panels.reshape(3, 1, PQ * BLOCK)
    (pay,) = call(pack_kernel, [(PAY, BLOCK)], nodes, flat, nu, vort, fetch=False)
    ring = range(PEERS)
    mate = lax.ppermute(pay, "blk", [(i, i ^ 1) for i in ring])
    block = pltpu.VMEM((BLOCK, BLOCK), BF16)
    line = (LINES, NJ)
    wide = (1, DEVS)
    own, send, pick, live = call(
        early_kernel,
        [line, (DEVS * FR, BLOCK), (DEVS * CAP, BLOCK), (DEVS * CAP, BLOCK)],
        flat,
        nodes,
        fringe_owner.reshape(wide),
        fringe_block.reshape(wide),
        fringe_size.reshape(wide),
        fringe_cell.reshape(wide),
        flow,
        scratch=(pltpu.VMEM((16, BLOCK), F32), block),
    )
    (near,) = call(join_kernel, [(NEAR, BLOCK)], pay, mate, own)

    def swap(mask):
        return lax.ppermute(near, "blk", [(i, i ^ mask) for i in ring])

    three = swap(6)
    two = swap(4)
    one = swap(2)
    (done,) = call(mate_kernel, [line], mate, nodes, own, scratch=(block,))
    ext = pltpu.VMEM((24, NJ), F32)
    dist, nu_next, send = call(
        step_kernel,
        [line, line, (DEVS * FR, BLOCK)],
        pay, mate, three, one, two, done, nodes, nu, vort, pick, live, send,
        scratch=(
            pltpu.VMEM((PEERS * BLOCK, BLOCK), BF16),
            pltpu.VMEM((3, 24, NJ), F32),
            ext, ext, ext,
        ),
        alias=((11, 2),),
        hbm=(0, 1),
    )
    got = exchange(send, DEVS, ("grp", "blk"), [[i ^ FLIP for i in range(DEVS)]])
    (offbody,) = call(sum_kernel, [(VARS, OB, BLOCK)], got, hbm=(0,))
    return (dist[None], nu_next[None], jnp.transpose(offbody, (1, 0, 2)))


def solution(mesh):
    in_specs = (
        P("grp", None, "blk", None),
        P("grp", None, "blk"),
        P("grp", "blk", None),
        P("grp", "blk", None),
        P("grp", None, "blk", None),
        P(("grp", "blk")),
        P(("grp", "blk")),
        P(("grp", "blk"), None),
        P(("grp", "blk")),
    )
    out_specs = (P("grp", "blk", None), P("grp", "blk", None), P(("grp", "blk"), None, None))
    return jax.shard_map(
        per_device, mesh=mesh, in_specs=in_specs, out_specs=out_specs, check_vma=False
    )
```

```python
import functools

import jax
import jax.numpy as jnp
from jax import lax
from jax.experimental import pallas as pl
from jax.experimental.pallas import tpu as pltpu
from jax.sharding import PartitionSpec as P

BLOCK = 128
VARS = 5
CAP = 2
OB = 16
PEERS = 8
DEVS = 128
LINES = 16
NJ = 256
PQ = 4
PAN = 12
EDGE = 12
PAY = 40
NEAR = 36
FR = 11
UNROLL = 16
OWN_UNROLL = 16
FLIP = 69
F32 = jnp.float32
BF16 = jnp.bfloat16


def iota(shape, axis):
    return lax.broadcasted_iota(jnp.int32, shape, axis)


def split3(v):
    high = v.astype(BF16)
    rest = v - high.astype(F32)
    mid = rest.astype(BF16)
    low = (rest - mid.astype(F32)).astype(BF16)
    return high, mid, low


def onehot(cond):
    return jnp.where(cond, 1.0, 0.0).astype(BF16)


def contract_lanes(a, b):
    return lax.dot_general(a, b, (((1,), (1,)), ((), ())), preferred_element_type=F32)


def halves(rows):
    return jnp.concatenate([rows[:, :BLOCK], rows[:, BLOCK:]], axis=0)


def pack_kernel(nodes_ref, panels_ref, nu_ref, vort_ref, out_ref):
    def put(row, value):
        out_ref[pl.ds(row, 1), :] = value

    for c in range(3):
        vec = panels_ref[c]
        for q in range(PQ):
            put(c * PQ + q, vec[:, q * BLOCK : (q + 1) * BLOCK])
    odd = lax.rem(lax.axis_index("blk"), 2)
    for base, nu_line, line in (
        (PAN + EDGE * (1 - odd), 0, 0),
        (PAN + EDGE * odd, LINES - 2, LINES - 1),
    ):
        for half in range(2):
            lanes = slice(half * BLOCK, (half + 1) * BLOCK)
            for at in range(2):
                put(base + at * 2 + half, nu_ref[nu_line + at : nu_line + at + 1, lanes])
            put(base + 4 + half, vort_ref[line : line + 1, lanes])
            for c in range(3):
                put(base + 6 + c * 2 + half, nodes_ref[c, line : line + 1, lanes])
    out_ref[PAN + 2 * EDGE :, :] = jnp.zeros((PAY - PAN - 2 * EDGE, BLOCK), F32)


def join_kernel(pay_ref, mate_ref, least_ref, near_ref):
    near_ref[0:PAN, :] = pay_ref[0:PAN, :]
    near_ref[PAN : 2 * PAN, :] = mate_ref[0:PAN, :]
    near_ref[2 * PAN : NEAR, :] = mate_ref[PAN + EDGE : PAN + 2 * EDGE, :]


def panel_terms(raw):
    square = raw[0:4] * raw[0:4] + raw[4:8] * raw[4:8] + raw[8:12] * raw[8:12]
    high, mid, low = [
        t.astype(F32) for t in split3(jnp.concatenate([raw, square], axis=0))
    ]
    none = jnp.zeros_like(high)
    terms = jnp.concatenate([high, high, high, mid, mid, low, none, none], axis=0)
    return terms.T.astype(BF16)


def line_least(coords, lhs):
    c4 = iota((PQ * 4, NJ), 0) // 4
    q4 = iota((PQ * 4, NJ), 0) % 4
    x, y, z = [jnp.broadcast_to(v, (PQ * 4, NJ)) for v in coords]
    base = jnp.where(c4 == 0, x, jnp.where(c4 == 1, y, z)) * -2.0
    base = jnp.where(c4 == 3, 1.0, base)
    best = None
    for q in range(PQ):
        high, mid, low = split3(jnp.where(q4 == q, base, 0.0))
        none = jnp.zeros_like(high)
        w = jnp.concatenate([high, mid, low, high, mid, high, none, none], axis=0)
        rest = jnp.dot(lhs, w, preferred_element_type=F32)
        least = jnp.min(rest.reshape(lhs.shape[0] // 8, 8, NJ), axis=0)
        best = least if best is None else jnp.minimum(best, least)
    return best


def lines_least(nodes_ref, lhs_ref, least_ref, before):
    def line(i, unused):
        best = line_least([nodes_ref[c, pl.ds(i, 1), :] for c in range(3)], lhs_ref[...])
        best = jnp.min(best, axis=0, keepdims=True)
        if before is not None:
            best = jnp.minimum(best, before[pl.ds(i, 1), :])
        least_ref[pl.ds(i, 1), :] = best
        return unused

    lax.fori_loop(0, LINES, line, 0, unroll=OWN_UNROLL)


def own_least(panels_ref, nodes_ref, least_ref, raw_ref, lhs_ref):
    for c in range(3):
        vec = panels_ref[c]
        for q in range(PQ):
            raw_ref[c * PQ + q : c * PQ + q + 1, :] = vec[:, q * BLOCK : (q + 1) * BLOCK]
    lhs_ref[...] = panel_terms(raw_ref[0:PAN, :])
    lines_least(nodes_ref, lhs_ref, least_ref, None)


def mate_kernel(pay_ref, mate_ref, nodes_ref, own_ref, least_ref, lhs_ref):
    lhs_ref[0:BLOCK, :] = panel_terms(mate_ref[0:PAN, :])
    lhs_ref[BLOCK:, :] = panel_terms(pay_ref[0:PAN, :])
    lines_least(nodes_ref, lhs_ref.at[0:BLOCK], least_ref, own_ref)
    edge = [
        jnp.concatenate([mate_ref[at : at + 1, :], mate_ref[at + 1 : at + 2, :]], axis=1)
        for at in range(PAN + 6, PAN + EDGE, 2)
    ]
    best = line_least(edge, lhs_ref[...])
    least_ref[LINES : LINES + 1, :] = jnp.min(best, axis=0, keepdims=True)


def early_kernel(
    panels_ref, nodes_ref, owner_ref, block_ref, size_ref, cell_ref, flow_ref,
    least_ref, send_ref, pick_ref, live_ref,
    raw_ref, lhs_ref,
):
    own_least(panels_ref, nodes_ref, least_ref, raw_ref, lhs_ref)
    square = (DEVS, DEVS)
    row = iota(square, 0)
    lane = iota(square, 1)
    owner = owner_ref[...]
    hits = onehot(jnp.broadcast_to(owner, square) == row)
    before = onehot(row < lane)
    earlier = jnp.dot(hits, before, preferred_element_type=F32)
    rank = jnp.sum(hits.astype(F32) * earlier, axis=0, keepdims=True)
    slot = (owner ^ FLIP) * CAP + rank.astype(jnp.int32)
    block = block_ref[...]
    place = (block % 2) * LINES + block // 2
    places = onehot((jnp.broadcast_to(place, square) == row % 32) & (row < 96))
    sizes = jnp.broadcast_to(size_ref[...], square).astype(F32).astype(BF16)
    cell = jnp.broadcast_to(cell_ref[...], square)
    state = jnp.concatenate([halves(flow_ref[v]) for v in range(VARS - 1)], axis=1)
    high, mid, low = split3(state)
    table = jnp.concatenate([high, mid, low, jnp.zeros_like(high)], axis=0)
    cells = None
    for r in range(CAP):
        sel = onehot(jnp.broadcast_to(slot, square) == row * CAP + r)
        pick = contract_lanes(sel, places)
        live = jnp.where(lane.astype(F32) < contract_lanes(sel, sizes), 1.0, 0.0)
        named = contract_lanes(sel, onehot((cell == row - r * OB) & (row < (r + 1) * OB)))
        cells = named if cells is None else cells + named
        pick_ref[pl.ds(r * DEVS, DEVS), :] = pick
        live_ref[pl.ds(r * DEVS, DEVS), :] = live
        values = jnp.dot(pick.astype(BF16), table, preferred_element_type=F32)
        for v in range(VARS - 1):
            send_ref[pl.ds(r * VARS + 1 + v, DEVS, stride=FR), :] = (
                values[:, v * BLOCK : (v + 1) * BLOCK] * live
            )
    send_ref[pl.ds(FR - 1, DEVS, stride=FR), :] = cells


def sa_step(centre, east, west, dist, vort):
    lane = iota(centre.shape, 1)
    north = jnp.where(lane == NJ - 1, 0.0, pltpu.roll(centre, NJ - 1, 1))
    south = jnp.where(lane == 0, 0.0, pltpu.roll(centre, 1, 1))
    flux = (1.0 + 0.5 * (centre + east)) * (east - centre) - (1.0 + 0.5 * (centre + west)) * (
        centre - west
    )
    flux = (
        flux
        + (1.0 + 0.5 * (centre + north)) * (north - centre)
        - (1.0 + 0.5 * (centre + south)) * (centre - south)
    )
    grads = 0.25 * ((east - west) * (east - west) + (north - south) * (north - south))
    diffusion = (flux + 0.622 * grads) * 1.5
    ratio = centre / dist
    return centre + 0.02 * (0.1355 * vort * centre - 3.24 * ratio * ratio + diffusion)


def step_kernel(
    pay_ref, mate_ref, three_ref, one_ref, two_ref, done_ref, nodes_ref, nu_ref, vort_ref, pick_ref, live_ref, rows_ref,
    dist_ref, next_ref, send_ref,
    lhs_ref, node_ext, nu_ext, vort_ext, dist_ext,
):
    me = lax.axis_index("blk")
    even = lax.rem(me, 2) == 0
    outer_in_one = lax.rem(me + me // 2, 2) == 1

    def edge(left, row):
        def lines(ref, at):
            return jnp.concatenate([ref[at : at + 1, :], ref[at + 1 : at + 2, :]], axis=1)

        outer = jnp.where(
            outer_in_one, lines(one_ref, 2 * PAN + row), lines(three_ref, 2 * PAN + row)
        )
        inner = lines(mate_ref, PAN + row)
        return jnp.where(even, outer, inner) if left else jnp.where(even, inner, outer)

    for c in range(3):
        node_ext[c, 1 : 1 + LINES, :] = nodes_ref[c]
        node_ext[c, 0:1, :] = edge(True, 6 + c * 2)
        node_ext[c, 1 + LINES : 2 + LINES, :] = edge(False, 6 + c * 2)
    nu_ext[2 : 2 + LINES, :] = nu_ref[...]
    vort_ext[1 : 1 + LINES, :] = vort_ref[...]
    for at in range(2):
        nu_ext[at : at + 1, :] = edge(True, at * 2)
        nu_ext[2 + LINES + at : 3 + LINES + at, :] = edge(False, at * 2)
    vort_ext[0:1, :] = edge(True, 4)
    vort_ext[1 + LINES : 2 + LINES, :] = edge(False, 4)

    sources = [(ref, at) for ref in (one_ref, two_ref, three_ref) for at in (0, PAN)]
    sources += [(pay_ref, 0), (mate_ref, 0)]
    for k, (ref, at) in enumerate(sources):
        lhs_ref[k * BLOCK : (k + 1) * BLOCK, :] = panel_terms(ref[at : at + PAN, :])

    def finish(i, least):
        x, y, z = [node_ext[c, pl.ds(i, 1), :] for c in range(3)]
        least = jnp.maximum(least + (x * x + y * y + z * z), 0.0)
        dist_ext[pl.ds(i, 1), :] = jnp.sqrt(least + 0.25)

    def coords(i):
        return [node_ext[c, pl.ds(i, 1), :] for c in range(3)]

    def line(i, unused):
        best = line_least(coords(i), lhs_ref[0 : (PEERS - 2) * BLOCK, :])
        best = jnp.minimum(jnp.min(best, axis=0, keepdims=True), done_ref[pl.ds(i - 1, 1), :])
        finish(i, best)
        return unused

    inner = jnp.where(even, 1 + LINES, 0)
    best = line_least(coords(inner), lhs_ref[0 : (PEERS - 2) * BLOCK, :])
    best = jnp.minimum(jnp.min(best, axis=0, keepdims=True), done_ref[LINES : LINES + 1, :])
    finish(inner, best)
    outer = 1 + LINES - inner
    finish(outer, jnp.min(line_least(coords(outer), lhs_ref[...]), axis=0, keepdims=True))
    lax.fori_loop(1, 1 + LINES, line, 0, unroll=UNROLL)

    mid_nu = sa_step(
        nu_ext[1 : 3 + LINES, :],
        nu_ext[2 : 4 + LINES, :],
        nu_ext[0 : 2 + LINES, :],
        dist_ext[0 : 2 + LINES, :],
        vort_ext[0 : 2 + LINES, :],
    )
    nu_ext[0 : 2 + LINES, :] = mid_nu
    dist = dist_ext[1 : 1 + LINES, :]
    new = sa_step(
        nu_ext[1 : 1 + LINES, :],
        nu_ext[2 : 2 + LINES, :],
        nu_ext[0:LINES, :],
        dist,
        vort_ref[...],
    )
    dist_ref[...] = dist
    next_ref[...] = new
    high, mid, low = split3(halves(new))
    table = jnp.concatenate([high, mid, low, jnp.zeros_like(high)], axis=0)
    values = jnp.dot(pick_ref[...].astype(BF16), table, preferred_element_type=F32)
    values = values * live_ref[...]
    for r in range(CAP):
        send_ref[pl.ds(r * VARS, DEVS, stride=FR), :] = values[r * DEVS : (r + 1) * DEVS]


def add_up(chosen, rows):
    total = None
    for part in split3(rows):
        term = jnp.dot(chosen, part, preferred_element_type=F32)
        total = term if total is None else total + term
    return total


def sum_kernel(got_ref, out_ref):
    cells = got_ref[pl.ds(FR - 1, DEVS, stride=FR), :].T
    chosen = jnp.concatenate([cells[r * OB : (r + 1) * OB] for r in range(CAP)], axis=1)
    chosen = chosen.astype(BF16)
    def rows_of(v):
        return jnp.concatenate(
            [got_ref[pl.ds(r * VARS + v, DEVS, stride=FR), :] for r in range(CAP)], axis=0
        )

    for v in range(0, VARS, 2):
        both = range(v, min(v + 2, VARS))
        sums = add_up(chosen, jnp.concatenate([rows_of(w) for w in both], axis=1))
        for n, w in enumerate(both):
            out_ref[w] = sums[:, n * BLOCK : (n + 1) * BLOCK]


def call(kernel, outs, *args, scratch=(), alias=(), hbm=(), fetch=True):
    if fetch:
        args = [pltpu.with_memory_space_constraint(a, pltpu.VMEM) for a in args]
    vmem = pl.BlockSpec(memory_space=pltpu.VMEM)
    return pl.pallas_call(
        kernel,
        out_shape=tuple(
            (jax.ShapeDtypeStruct if n in hbm else pltpu.VMEM)(shape, F32)
            for n, shape in enumerate(outs)
        ),
        in_specs=[vmem] * len(args),
        out_specs=tuple(vmem for shape in outs),
        scratch_shapes=list(scratch),
        input_output_aliases=dict(alias),
    )(*args)


def exchange(rows, count, axes, groups=None):
    sent = rows.reshape(count, 1, -1)
    got = lax.all_to_all(sent, axes, split_axis=0, concat_axis=0, tiled=True, axis_index_groups=groups)
    return got.reshape(rows.shape)


def per_device(
    nodes, panels, nu_field, vorticity, flow, fringe_block, fringe_size, fringe_owner, fringe_cell
):
    nodes, nu, vort, flow = nodes[0], nu_field[0], vorticity[0], flow[0]
    flat = panels.reshape(3, 1, PQ * BLOCK)
    (pay,) = call(pack_kernel, [(PAY, BLOCK)], nodes, flat, nu, vort, fetch=False)
    ring = range(PEERS)
    mate = lax.ppermute(pay, "blk", [(i, i ^ 1) for i in ring])
    block = pltpu.VMEM((BLOCK, BLOCK), BF16)
    line = (LINES, NJ)
    wide = (1, DEVS)
    own, send, pick, live = call(
        early_kernel,
        [line, (DEVS * FR, BLOCK), (DEVS * CAP, BLOCK), (DEVS * CAP, BLOCK)],
        flat,
        nodes,
        fringe_owner.reshape(wide),
        fringe_block.reshape(wide),
        fringe_size.reshape(wide),
        fringe_cell.reshape(wide),
        flow,
        scratch=(pltpu.VMEM((16, BLOCK), F32), block),
    )
    (near,) = call(join_kernel, [(NEAR, BLOCK)], pay, mate, own)

    def swap(mask):
        return lax.ppermute(near, "blk", [(i, i ^ mask) for i in ring])

    three = swap(6)
    two = swap(4)
    one = swap(2)
    (done,) = call(
        mate_kernel, [(24, NJ)], pay, mate, nodes, own, scratch=(pltpu.VMEM((2 * BLOCK, BLOCK), BF16),)
    )
    ext = pltpu.VMEM((24, NJ), F32)
    dist, nu_next, send = call(
        step_kernel,
        [line, line, (DEVS * FR, BLOCK)],
        pay, mate, three, one, two, done, nodes, nu, vort, pick, live, send,
        scratch=(
            pltpu.VMEM((PEERS * BLOCK, BLOCK), BF16),
            pltpu.VMEM((3, 24, NJ), F32),
            ext, ext, ext,
        ),
        alias=((11, 2),),
        hbm=(0, 1),
    )
    got = exchange(send, DEVS, ("grp", "blk"), [[i ^ FLIP for i in range(DEVS)]])
    (offbody,) = call(sum_kernel, [(VARS, OB, BLOCK)], got, hbm=(0,))
    return (dist[None], nu_next[None], jnp.transpose(offbody, (1, 0, 2)))


def solution(mesh):
    in_specs = (
        P("grp", None, "blk", None),
        P("grp", None, "blk"),
        P("grp", "blk", None),
        P("grp", "blk", None),
        P("grp", None, "blk", None),
        P(("grp", "blk")),
        P(("grp", "blk")),
        P(("grp", "blk"), None),
        P(("grp", "blk")),
    )
    out_specs = (P("grp", "blk", None), P("grp", "blk", None), P(("grp", "blk"), None, None))
    return jax.shard_map(
        per_device, mesh=mesh, in_specs=in_specs, out_specs=out_specs, check_vma=False
    )
```

```python
import functools

import jax
import jax.numpy as jnp
from jax import lax
from jax.experimental import pallas as pl
from jax.experimental.pallas import tpu as pltpu
from jax.sharding import PartitionSpec as P

BLOCK = 128
VARS = 5
CAP = 2
OB = 16
PEERS = 8
DEVS = 128
LINES = 16
NJ = 256
PQ = 4
PAN = 12
EDGE = 12
PAY = 40
NEAR = 36
FR = 11
UNROLL = 16
OWN_UNROLL = 16
FLIP = 69
F32 = jnp.float32
BF16 = jnp.bfloat16


def iota(shape, axis):
    return lax.broadcasted_iota(jnp.int32, shape, axis)


def split3(v):
    high = v.astype(BF16)
    rest = v - high.astype(F32)
    mid = rest.astype(BF16)
    low = (rest - mid.astype(F32)).astype(BF16)
    return high, mid, low


def onehot(cond):
    return jnp.where(cond, 1.0, 0.0).astype(BF16)


def contract_lanes(a, b):
    return lax.dot_general(a, b, (((1,), (1,)), ((), ())), preferred_element_type=F32)


def halves(rows):
    return jnp.concatenate([rows[:, :BLOCK], rows[:, BLOCK:]], axis=0)


def pack_kernel(nodes_ref, panels_ref, nu_ref, vort_ref, out_ref):
    def put(row, value):
        out_ref[pl.ds(row, 1), :] = value

    for c in range(3):
        vec = panels_ref[c]
        for q in range(PQ):
            put(c * PQ + q, vec[:, q * BLOCK : (q + 1) * BLOCK])
    odd = lax.rem(lax.axis_index("blk"), 2)
    for base, nu_line, line in (
        (PAN + EDGE * (1 - odd), 0, 0),
        (PAN + EDGE * odd, LINES - 2, LINES - 1),
    ):
        for half in range(2):
            lanes = slice(half * BLOCK, (half + 1) * BLOCK)
            for at in range(2):
                put(base + at * 2 + half, nu_ref[nu_line + at : nu_line + at + 1, lanes])
            put(base + 4 + half, vort_ref[line : line + 1, lanes])
            for c in range(3):
                put(base + 6 + c * 2 + half, nodes_ref[c, line : line + 1, lanes])
    out_ref[PAN + 2 * EDGE :, :] = jnp.zeros((PAY - PAN - 2 * EDGE, BLOCK), F32)


def join_kernel(pay_ref, mate_ref, least_ref, near_ref):
    near_ref[0:PAN, :] = pay_ref[0:PAN, :]
    near_ref[PAN : 2 * PAN, :] = mate_ref[0:PAN, :]
    near_ref[2 * PAN : NEAR, :] = mate_ref[PAN + EDGE : PAN + 2 * EDGE, :]


def panel_terms(raw):
    square = raw[0:4] * raw[0:4] + raw[4:8] * raw[4:8] + raw[8:12] * raw[8:12]
    high, mid, low = [
        t.astype(F32) for t in split3(jnp.concatenate([raw, square], axis=0))
    ]
    none = jnp.zeros_like(high)
    terms = jnp.concatenate([high, high, high, mid, mid, low, none, none], axis=0)
    return terms.T.astype(BF16)


def line_least(coords, lhs):
    c4 = iota((PQ * 4, NJ), 0) // 4
    q4 = iota((PQ * 4, NJ), 0) % 4
    x, y, z = [jnp.broadcast_to(v, (PQ * 4, NJ)) for v in coords]
    base = jnp.where(c4 == 0, x, jnp.where(c4 == 1, y, z)) * -2.0
    base = jnp.where(c4 == 3, 1.0, base)
    best = None
    for q in range(PQ):
        high, mid, low = split3(jnp.where(q4 == q, base, 0.0))
        none = jnp.zeros_like(high)
        w = jnp.concatenate([high, mid, low, high, mid, high, none, none], axis=0)
        rest = jnp.dot(lhs, w, preferred_element_type=F32)
        least = jnp.min(rest.reshape(lhs.shape[0] // 8, 8, NJ), axis=0)
        best = least if best is None else jnp.minimum(best, least)
    return best


def lines_least(nodes_ref, lhs_ref, least_ref, before):
    def line(i, unused):
        best = line_least([nodes_ref[c, pl.ds(i, 1), :] for c in range(3)], lhs_ref[...])
        best = jnp.min(best, axis=0, keepdims=True)
        if before is not None:
            best = jnp.minimum(best, before[pl.ds(i, 1), :])
        least_ref[pl.ds(i, 1), :] = best
        return unused

    lax.fori_loop(0, LINES, line, 0, unroll=OWN_UNROLL)


def own_least(panels_ref, nodes_ref, least_ref, raw_ref, lhs_ref):
    for c in range(3):
        vec = panels_ref[c]
        for q in range(PQ):
            raw_ref[c * PQ + q : c * PQ + q + 1, :] = vec[:, q * BLOCK : (q + 1) * BLOCK]
    lhs_ref[...] = panel_terms(raw_ref[0:PAN, :])
    lines_least(nodes_ref, lhs_ref, least_ref, None)


def mate_kernel(pay_ref, mate_ref, nodes_ref, own_ref, least_ref, lhs_ref):
    lhs_ref[0:BLOCK, :] = panel_terms(mate_ref[0:PAN, :])
    lhs_ref[BLOCK:, :] = panel_terms(pay_ref[0:PAN, :])
    lines_least(nodes_ref, lhs_ref.at[0:BLOCK], least_ref, own_ref)
    edge = [
        jnp.concatenate([mate_ref[at : at + 1, :], mate_ref[at + 1 : at + 2, :]], axis=1)
        for at in range(PAN + 6, PAN + EDGE, 2)
    ]
    best = line_least(edge, lhs_ref[...])
    least_ref[LINES : LINES + 1, :] = jnp.min(best, axis=0, keepdims=True)


def early_kernel(
    panels_ref, nodes_ref, owner_ref, block_ref, size_ref, cell_ref, flow_ref,
    least_ref, send_ref, pick_ref, live_ref,
    raw_ref, lhs_ref,
):
    own_least(panels_ref, nodes_ref, least_ref, raw_ref, lhs_ref)
    square = (DEVS, DEVS)
    row = iota(square, 0)
    lane = iota(square, 1)
    owner = owner_ref[...]
    hits = onehot(jnp.broadcast_to(owner, square) == row)
    before = onehot(row < lane)
    earlier = jnp.dot(hits, before, preferred_element_type=F32)
    rank = jnp.sum(hits.astype(F32) * earlier, axis=0, keepdims=True)
    slot = (owner ^ FLIP) * CAP + rank.astype(jnp.int32)
    block = block_ref[...]
    place = (block % 2) * LINES + block // 2
    places = onehot((jnp.broadcast_to(place, square) == row % 32) & (row < 96))
    sizes = jnp.broadcast_to(size_ref[...], square).astype(F32).astype(BF16)
    cell = jnp.broadcast_to(cell_ref[...], square)
    state = jnp.concatenate([halves(flow_ref[v]) for v in range(VARS - 1)], axis=1)
    high, mid, low = split3(state)
    table = jnp.concatenate([high, mid, low, jnp.zeros_like(high)], axis=0)
    cells = None
    for r in range(CAP):
        sel = onehot(jnp.broadcast_to(slot, square) == row * CAP + r)
        pick = contract_lanes(sel, places)
        live = jnp.where(lane.astype(F32) < contract_lanes(sel, sizes), 1.0, 0.0)
        named = contract_lanes(sel, onehot((cell == row - r * OB) & (row < (r + 1) * OB)))
        cells = named if cells is None else cells + named
        pick_ref[pl.ds(r * DEVS, DEVS), :] = pick
        live_ref[pl.ds(r * DEVS, DEVS), :] = live
        values = jnp.dot(pick.astype(BF16), table, preferred_element_type=F32)
        for v in range(VARS - 1):
            send_ref[pl.ds(r * VARS + 1 + v, DEVS, stride=FR), :] = (
                values[:, v * BLOCK : (v + 1) * BLOCK] * live
            )
    send_ref[pl.ds(FR - 1, DEVS, stride=FR), :] = cells


def sa_step(centre, east, west, dist, vort):
    lane = iota(centre.shape, 1)
    north = jnp.where(lane == NJ - 1, 0.0, pltpu.roll(centre, NJ - 1, 1))
    south = jnp.where(lane == 0, 0.0, pltpu.roll(centre, 1, 1))
    flux = (1.0 + 0.5 * (centre + east)) * (east - centre) - (1.0 + 0.5 * (centre + west)) * (
        centre - west
    )
    flux = (
        flux
        + (1.0 + 0.5 * (centre + north)) * (north - centre)
        - (1.0 + 0.5 * (centre + south)) * (centre - south)
    )
    grads = 0.25 * ((east - west) * (east - west) + (north - south) * (north - south))
    diffusion = (flux + 0.622 * grads) * 1.5
    ratio = centre / dist
    return centre + 0.02 * (0.1355 * vort * centre - 3.24 * ratio * ratio + diffusion)


def step_kernel(
    pair_ref, mate_ref, three_ref, one_ref, two_ref, done_ref, nodes_ref, nu_ref, vort_ref, pick_ref, live_ref, rows_ref,
    dist_ref, next_ref, send_ref,
    lhs_ref, node_ext, nu_ext, vort_ext, dist_ext,
):
    me = lax.axis_index("blk")
    even = lax.rem(me, 2) == 0
    outer_in_one = lax.rem(me + me // 2, 2) == 1

    def edge(left, row):
        def lines(ref, at):
            return jnp.concatenate([ref[at : at + 1, :], ref[at + 1 : at + 2, :]], axis=1)

        outer = jnp.where(
            outer_in_one, lines(one_ref, 2 * PAN + row), lines(three_ref, 2 * PAN + row)
        )
        inner = lines(mate_ref, PAN + row)
        return jnp.where(even, outer, inner) if left else jnp.where(even, inner, outer)

    for c in range(3):
        node_ext[c, 1 : 1 + LINES, :] = nodes_ref[c]
        node_ext[c, 0:1, :] = edge(True, 6 + c * 2)
        node_ext[c, 1 + LINES : 2 + LINES, :] = edge(False, 6 + c * 2)
    nu_ext[2 : 2 + LINES, :] = nu_ref[...]
    vort_ext[1 : 1 + LINES, :] = vort_ref[...]
    for at in range(2):
        nu_ext[at : at + 1, :] = edge(True, at * 2)
        nu_ext[2 + LINES + at : 3 + LINES + at, :] = edge(False, at * 2)
    vort_ext[0:1, :] = edge(True, 4)
    vort_ext[1 + LINES : 2 + LINES, :] = edge(False, 4)

    sources = [(ref, at) for ref in (one_ref, two_ref, three_ref) for at in (0, PAN)]
    for k, (ref, at) in enumerate(sources):
        lhs_ref[k * BLOCK : (k + 1) * BLOCK, :] = panel_terms(ref[at : at + PAN, :])

    def finish(i, least):
        x, y, z = [node_ext[c, pl.ds(i, 1), :] for c in range(3)]
        least = jnp.maximum(least + (x * x + y * y + z * z), 0.0)
        dist_ext[pl.ds(i, 1), :] = jnp.sqrt(least + 0.25)

    def coords(i):
        return [node_ext[c, pl.ds(i, 1), :] for c in range(3)]

    def line(i, unused):
        best = line_least(coords(i), lhs_ref[...])
        best = jnp.minimum(jnp.min(best, axis=0, keepdims=True), done_ref[pl.ds(i - 1, 1), :])
        finish(i, best)
        return unused

    inner = jnp.where(even, 1 + LINES, 0)
    best = line_least(coords(inner), lhs_ref[...])
    best = jnp.minimum(jnp.min(best, axis=0, keepdims=True), done_ref[LINES : LINES + 1, :])
    finish(inner, best)
    outer = 1 + LINES - inner
    best = jnp.minimum(line_least(coords(outer), lhs_ref[...]), line_least(coords(outer), pair_ref[...]))
    finish(outer, jnp.min(best, axis=0, keepdims=True))
    lax.fori_loop(1, 1 + LINES, line, 0, unroll=UNROLL)

    mid_nu = sa_step(
        nu_ext[1 : 3 + LINES, :],
        nu_ext[2 : 4 + LINES, :],
        nu_ext[0 : 2 + LINES, :],
        dist_ext[0 : 2 + LINES, :],
        vort_ext[0 : 2 + LINES, :],
    )
    nu_ext[0 : 2 + LINES, :] = mid_nu
    dist = dist_ext[1 : 1 + LINES, :]
    new = sa_step(
        nu_ext[1 : 1 + LINES, :],
        nu_ext[2 : 2 + LINES, :],
        nu_ext[0:LINES, :],
        dist,
        vort_ref[...],
    )
    dist_ref[...] = dist
    next_ref[...] = new
    high, mid, low = split3(halves(new))
    table = jnp.concatenate([high, mid, low, jnp.zeros_like(high)], axis=0)
    values = jnp.dot(pick_ref[...].astype(BF16), table, preferred_element_type=F32)
    values = values * live_ref[...]
    for r in range(CAP):
        send_ref[pl.ds(r * VARS, DEVS, stride=FR), :] = values[r * DEVS : (r + 1) * DEVS]


def add_up(chosen, rows):
    total = None
    for part in split3(rows):
        term = jnp.dot(chosen, part, preferred_element_type=F32)
        total = term if total is None else total + term
    return total


def sum_kernel(got_ref, out_ref):
    cells = got_ref[pl.ds(FR - 1, DEVS, stride=FR), :].T
    chosen = jnp.concatenate([cells[r * OB : (r + 1) * OB] for r in range(CAP)], axis=1)
    chosen = chosen.astype(BF16)
    def rows_of(v):
        return jnp.concatenate(
            [got_ref[pl.ds(r * VARS + v, DEVS, stride=FR), :] for r in range(CAP)], axis=0
        )

    for v in range(0, VARS, 2):
        both = range(v, min(v + 2, VARS))
        sums = add_up(chosen, jnp.concatenate([rows_of(w) for w in both], axis=1))
        for n, w in enumerate(both):
            out_ref[w] = sums[:, n * BLOCK : (n + 1) * BLOCK]


def call(kernel, outs, *args, scratch=(), alias=(), hbm=(), fetch=True, types=()):
    if fetch:
        args = [pltpu.with_memory_space_constraint(a, pltpu.VMEM) for a in args]
    vmem = pl.BlockSpec(memory_space=pltpu.VMEM)
    return pl.pallas_call(
        kernel,
        out_shape=tuple(
            (jax.ShapeDtypeStruct if n in hbm else pltpu.VMEM)(shape, dict(types).get(n, F32))
            for n, shape in enumerate(outs)
        ),
        in_specs=[vmem] * len(args),
        out_specs=tuple(vmem for shape in outs),
        scratch_shapes=list(scratch),
        input_output_aliases=dict(alias),
    )(*args)


def exchange(rows, count, axes, groups=None):
    sent = rows.reshape(count, 1, -1)
    got = lax.all_to_all(sent, axes, split_axis=0, concat_axis=0, tiled=True, axis_index_groups=groups)
    return got.reshape(rows.shape)


def per_device(
    nodes, panels, nu_field, vorticity, flow, fringe_block, fringe_size, fringe_owner, fringe_cell
):
    nodes, nu, vort, flow = nodes[0], nu_field[0], vorticity[0], flow[0]
    flat = panels.reshape(3, 1, PQ * BLOCK)
    (pay,) = call(pack_kernel, [(PAY, BLOCK)], nodes, flat, nu, vort, fetch=False)
    ring = range(PEERS)
    mate = lax.ppermute(pay, "blk", [(i, i ^ 1) for i in ring])
    block = pltpu.VMEM((BLOCK, BLOCK), BF16)
    line = (LINES, NJ)
    wide = (1, DEVS)
    own, send, pick, live = call(
        early_kernel,
        [line, (DEVS * FR, BLOCK), (DEVS * CAP, BLOCK), (DEVS * CAP, BLOCK)],
        flat,
        nodes,
        fringe_owner.reshape(wide),
        fringe_block.reshape(wide),
        fringe_size.reshape(wide),
        fringe_cell.reshape(wide),
        flow,
        scratch=(pltpu.VMEM((16, BLOCK), F32), block),
    )
    (near,) = call(join_kernel, [(NEAR, BLOCK)], pay, mate, own)

    def swap(mask):
        return lax.ppermute(near, "blk", [(i, i ^ mask) for i in ring])

    three = swap(6)
    two = swap(4)
    one = swap(2)
    done, pair_terms = call(
        mate_kernel,
        [(24, NJ), (2 * BLOCK, BLOCK)],
        pay, mate, nodes, own,
        types=((1, BF16),),
    )
    ext = pltpu.VMEM((24, NJ), F32)
    dist, nu_next, send = call(
        step_kernel,
        [line, line, (DEVS * FR, BLOCK)],
        pair_terms, mate, three, one, two, done, nodes, nu, vort, pick, live, send,
        scratch=(
            pltpu.VMEM(((PEERS - 2) * BLOCK, BLOCK), BF16),
            pltpu.VMEM((3, 24, NJ), F32),
            ext, ext, ext,
        ),
        alias=((11, 2),),
        hbm=(0, 1),
    )
    got = exchange(send, DEVS, ("grp", "blk"), [[i ^ FLIP for i in range(DEVS)]])
    (offbody,) = call(sum_kernel, [(VARS, OB, BLOCK)], got, hbm=(0,))
    return (dist[None], nu_next[None], jnp.transpose(offbody, (1, 0, 2)))


def solution(mesh):
    in_specs = (
        P("grp", None, "blk", None),
        P("grp", None, "blk"),
        P("grp", "blk", None),
        P("grp", "blk", None),
        P("grp", None, "blk", None),
        P(("grp", "blk")),
        P(("grp", "blk")),
        P(("grp", "blk"), None),
        P(("grp", "blk")),
    )
    out_specs = (P("grp", "blk", None), P("grp", "blk", None), P(("grp", "blk"), None, None))
    return jax.shard_map(
        per_device, mesh=mesh, in_specs=in_specs, out_specs=out_specs, check_vma=False
    )
```
